32 devices in a mesh: concept: 8 (over y, x, core), group: 4 (over z).
Axes of the slice: x: 2, y: 2, z: 4, core: 2. Of those that a mesh axis runs over, the one named last changes fastest.
Arguments:
- latents: bfloat16 [32, 48, 64], P(('concept', 'group')), may hold values from -6 to 6
- concept_lists: int32 [32, 3], replicated, may hold values from 0 to 7, all different within a row; in each aligned block of 1 rows (0 to 0, 1 to 1, ...) no two rows name the same one
- list_length: int32 [32], replicated, may hold values from 1 to 3
- concept_owner: int32 [8], replicated, may hold values from 0 to 7, each once
- strength: float32 [32], P(('concept', 'group')), may hold values from 10 to 40
- embed: bfloat16 [8, 64, 1024], P('concept'), may hold values from -0.75 to 0.75
- gain_in: float32 [8, 1024], P('concept'), may hold values from 0.25 to 1.75
- w_up: bfloat16 [8, 1024, 2048], P('concept', None, 'group'), may hold values from -0.1875 to 0.1875
- w_down: bfloat16 [8, 2048, 1024], P('concept', 'group'), may hold values from -0.125 to 0.125
- gain_out: float32 [8, 1024], P('concept'), may hold values from 0.25 to 1.75
- w_head: float32 [8, 1024], P('concept'), may hold values from -4 to 4
Outputs:
- guidance: float32 [32, 48, 64], P(('concept', 'group'))
The draws below stay inside these ranges and needn't reach their ends.
Inputs may be any that keep to these rules, and one draw needn't show every extreme that they name: `concept_lists`: entries of one row are distinct; a device's single image names each concept at most once. `concept_owner`: each classifier index appears exactly once.
All inputs are finite; a program needn't handle non-finite values.
Results may differ from the reference program's by a relative error of at most 0.0046.
Values may be sent and summed in bfloat16 or wider, within the bound.
A program may use at most 64 MiB of HBM per device.

```python
import math
import jax
import jax.numpy as jnp
import numpy as np
from jax import lax

D = 1024
FF = 2048
C = 64
TOPC = 3
IMG_DEV = 1
PATCHES = 48
CONCEPTS = 8
IMAGES = 32
CAP = 1


def with_ends(array, stream_key, low, high):
    dims = array.shape
    index_at = [jax.random.randint(jax.random.fold_in(stream_key, axis), (), 0, dims[axis]) for axis in range(len(dims))]
    array = array.at[tuple(index_at)].set(low)
    longest = dims.index(max(dims))
    index_at[longest] = (index_at[longest] + 1) % dims[longest]
    return array.at[tuple(index_at)].set(high)


def shard_levels(stream_key, shape, cuts, smallest, high):
    factor_of, own = 1.0, jax.random.fold_in(stream_key, 6)
    for position, parts in cuts:
        steps = jnp.exp(jax.random.uniform(jax.random.fold_in(own, position), (parts,), jnp.float32, smallest / len(cuts), high / len(cuts)))
        factor_of = factor_of * jnp.repeat(steps, shape[position] // parts).reshape([-1 if axis == position else 1 for axis in range(len(shape))])
    return factor_of


def shared_out(own_key, own, number, rows, amount, top, reach, lean):
    order = jax.random.permutation(own_key, amount)
    crowded, usual = load_shares(amount, rows * top, reach, lean, True), load_shares(amount, rows * top, reach, lean, False)
    places = jnp.arange(amount)

    def named(sizes, rotation):
        used = int((sizes > 0).sum())
        fixed = max(1, used // 4)
        moved = fixed + (places - fixed + rotation * (used - fixed)) % max(1, amount - fixed)
        return jnp.zeros((amount,), jnp.int32).at[order[jnp.where(places < fixed, places, moved)]].set(jnp.asarray(sizes, jnp.int32))

    sizes = jnp.where(number % 4 == 0, named(crowded, number // 4), named(usual, number - number // 4 - 1))
    mixed = jax.random.permutation(jax.random.fold_in(own, 3), amount)
    giver, sink = mixed[0:amount // 2 * 2:2], mixed[1:amount // 2 * 2:2]
    room = jnp.minimum(sizes[giver] - 1, reach - sizes[sink]) // 2
    room = jnp.where((giver == order[0]) | (sink == order[0]) | (sizes[sink] == 0), 0, jnp.maximum(room, 0))
    moved = jax.random.randint(jax.random.fold_in(own, 4), (amount // 2,), 0, 1 << 20) % (room + 1)
    sizes = sizes.at[giver].add(-moved).at[sink].add(moved)
    labels = jnp.searchsorted(jnp.cumsum(sizes), jnp.arange(rows * top), side="right").astype(jnp.int32)
    grid = labels.reshape(top, rows).T
    grid = grid[jax.random.permutation(jax.random.fold_in(own, 1), rows)]
    rotation = jax.random.randint(jax.random.fold_in(own, 2), (rows, 1), 0, top)
    return jnp.take_along_axis(grid, (jnp.arange(top)[None, :] + rotation) % top, axis=1)


def load_shares(amount, total, bound, lean, full):
    weights = [(1 << 20) // math.isqrt(standing ** lean) + 1 for standing in range(1, amount + 1)]
    largest = bound if full else min(bound, max(-(-total // amount), total * weights[0] // sum(weights)))
    least = 1 if total - largest >= amount - 1 else 0
    given, rest = [largest] + [least] * (amount - 1), total - largest - least * (amount - 1)
    while rest > 0:
        candidates = [i for i in range(1, amount) if given[i] < largest] or [i for i in range(1, amount) if given[i] < bound]
        mass, budget = sum([weights[i] for i in candidates]), rest
        for i in candidates:
            extra = min(bound - given[i], max(1, budget * weights[i] // mass), rest)
            given[i] = given[i] + extra
            rest = rest - extra
    return np.array(given)


def centred(key, shape, deviation, bound, cuts=(), held_as=jnp.bfloat16):
    result = deviation * jax.random.normal(key, shape, jnp.float32)
    if cuts:
        result = result * shard_levels(key, shape, cuts, -0.22, 0.18)
    return jnp.clip(result, -bound, bound).astype(held_as)


def setup_inputs(seed: int = 0) -> dict:
    key_list = jax.random.split(jax.random.key(seed), 12)
    latents = centred(key_list[0], (IMAGES, PATCHES, C), 1.0, 6.0, ((0, 32),))
    concept_lists_keys = jax.random.split(jax.random.fold_in(key_list[1], 1), IMAGES // IMG_DEV)
    concept_lists_turns = jax.random.permutation(jax.random.fold_in(key_list[1], 3), IMAGES // IMG_DEV)
    concept_lists = jax.vmap(lambda own, number: shared_out(jax.random.fold_in(key_list[1], 2), own, number, IMG_DEV, CONCEPTS, TOPC, CAP, 2))(concept_lists_keys, concept_lists_turns).reshape((IMAGES, TOPC))
    list_length = with_ends(jax.random.randint(key_list[2], (IMAGES,), 1, TOPC + 1), jax.random.fold_in(key_list[2], 1), 1, TOPC).astype(jnp.int32)
    concept_owner = jax.random.permutation(key_list[3], CONCEPTS).astype(jnp.int32)
    strength = jnp.clip(jnp.exp(math.log(40.0) - 1.3862944 * jax.random.uniform(key_list[4], (IMAGES,), jnp.float32) ** shard_levels(key_list[4], (IMAGES,), ((0, 32),), -0.2, 0.2)), 10.0, 40.0)
    embed = centred(key_list[5], (CONCEPTS, C, D), C ** -0.5, 0.75, ((0, 8),))
    gain_in = jnp.clip(1.0 + 0.15 * jax.random.normal(key_list[6], (CONCEPTS, D), jnp.float32), 0.25, 1.75)
    w_up = centred(key_list[7], (CONCEPTS, D, FF), D ** -0.5, 0.1875, ((0, 8), (2, 4)))
    w_down = centred(key_list[8], (CONCEPTS, FF, D), FF ** -0.5, 0.125, ((0, 8), (1, 4)))
    gain_out = jnp.clip(1.0 + 0.15 * jax.random.normal(key_list[9], (CONCEPTS, D), jnp.float32), 0.25, 1.75)
    w_head = centred(key_list[10], (CONCEPTS, D), 1.0, 4.0, ((0, 8),), jnp.float32)
    return dict(latents=latents, concept_lists=concept_lists, list_length=list_length, concept_owner=concept_owner, strength=strength, embed=embed, gain_in=gain_in, w_up=w_up, w_down=w_down, gain_out=gain_out, w_head=w_head)


def norm_forward(values):
    center = lax.optimization_barrier(jnp.mean(values, axis=-1, keepdims=True))
    shifted = values - center
    variance = lax.optimization_barrier(jnp.mean(shifted * shifted, axis=-1, keepdims=True))
    inverse = lax.rsqrt(variance + 1e-05)
    return (shifted * inverse, inverse)

def norm_backward(upstream, normed, inverse):
    return inverse * (upstream - lax.optimization_barrier(jnp.mean(upstream, axis=-1, keepdims=True)) - normed * lax.optimization_barrier(jnp.mean(upstream * normed, axis=-1, keepdims=True)))

def gelu_pair(pre_act):
    cumulative = 0.5 * (1.0 + lax.erf(pre_act * 0.7071067811865476))
    return (pre_act * cumulative, cumulative + pre_act * jnp.exp(-0.5 * pre_act * pre_act) * 0.3989422804014327)

def pair_gradient(image, embed_one, gain_first, up_one, down_one, gain_last, head_one):
    base = jnp.dot(image, embed_one, preferred_element_type=jnp.float32)
    normed_in, inverse_in = norm_forward(base)
    scaled = (normed_in * gain_first).astype(jnp.bfloat16)
    pre_act = jnp.dot(scaled, up_one, preferred_element_type=jnp.float32)
    activated, slopes = gelu_pair(pre_act)
    hidden = activated.astype(jnp.bfloat16)
    residual = base + jnp.dot(hidden, down_one, preferred_element_type=jnp.float32)
    normed_out, inverse_out = norm_forward(residual)
    head_terms = normed_out * gain_last * head_one
    logit = jnp.sum(head_terms) / PATCHES
    factor = jax.nn.sigmoid(-logit) / PATCHES
    upstream = jnp.broadcast_to(factor * (head_one * gain_last), residual.shape)
    back_res = norm_backward(upstream, normed_out, inverse_out)
    back_res_b = back_res.astype(jnp.bfloat16)
    back_hidden = (jnp.dot(back_res_b, down_one.T, preferred_element_type=jnp.float32) * slopes).astype(jnp.bfloat16)
    back_scaled = jnp.dot(back_hidden, up_one.T, preferred_element_type=jnp.float32)
    back_base = (back_res + norm_backward(back_scaled * gain_first, normed_in, inverse_in)).astype(jnp.bfloat16)
    return jnp.dot(back_base, embed_one.T, preferred_element_type=jnp.float32)

def reference(latents, concept_lists, list_length, concept_owner, strength, embed, gain_in, w_up, w_down, gain_out, w_head):

    def one_image(packed):
        image, lists, length, scale = packed
        summed = jnp.zeros((PATCHES, C), jnp.float32)
        for entry in range(TOPC):
            owner = concept_owner[lists[entry]]
            grads = pair_gradient(image, embed[owner], gain_in[owner], w_up[owner], w_down[owner], gain_out[owner], w_head[owner])
            summed = summed + jnp.where(entry < length, grads, jnp.zeros_like(grads))
        return summed * scale
    return lax.map(one_image, (latents, concept_lists, list_length, strength))
```

```python
import functools

import jax
import jax.numpy as jnp
from jax import lax
from jax.experimental import pallas as pl
from jax.experimental.pallas import tpu as pltpu
from jax.sharding import PartitionSpec as P


def norm_forward(values):
    center = jnp.mean(values, axis=-1, keepdims=True)
    shifted = values - center
    variance = jnp.mean(shifted * shifted, axis=-1, keepdims=True)
    inverse = lax.rsqrt(variance + 1e-05)
    return (shifted * inverse, inverse)


def norm_backward(upstream, normed, inverse):
    return inverse * (
        upstream
        - jnp.mean(upstream, axis=-1, keepdims=True)
        - normed * jnp.mean(upstream * normed, axis=-1, keepdims=True)
    )


def gelu_pair(pre_act):
    cumulative = 0.5 * (1.0 + lax.erf(pre_act * 0.7071067811865476))
    return (
        pre_act * cumulative,
        cumulative + pre_act * jnp.exp(-0.5 * pre_act * pre_act) * 0.3989422804014327,
    )


def entry_owners(lists, lengths, owner_table):
    concept_ids = jnp.arange(owner_table.shape[0], dtype=jnp.int32)
    owners = jnp.sum(jnp.where(lists[:, :, None] == concept_ids, owner_table, 0), axis=2)
    active = jnp.arange(lists.shape[1], dtype=jnp.int32)[None, :] < lengths[:, None]
    return (owners, active)


def contract_last(left, right):
    return lax.dot_general(
        left, right, (((1,), (1,)), ((), ())), preferred_element_type=jnp.float32
    )


PER_CHUNK = 2


def guide_kernel(
    chunks,
    members,
    shares,
    slot_ref,
    back_slot_ref,
    back_mask_ref,
    strength_ref,
    latent_ref,
    embed_ref,
    gain_in_ref,
    up_ref,
    down_ref,
    gain_out_ref,
    head_ref,
    out_ref,
    lat,
    whole,
    normed,
    inverse,
    slopes,
    own,
    to_right,
    to_left,
    from_left,
    from_right,
    grads,
    spread,
    met,
    column,
    ends,
    lat_send,
    lat_recv,
    line_send,
    line_recv,
    right_send,
    right_recv,
    left_send,
    left_recv,
    back_send,
    back_recv,
    end_send,
    end_recv,
):
    c = lax.axis_index("concept")
    g = lax.axis_index("group")
    patches = latent_ref.shape[1]
    concept_peers = [lax.rem(c + k, members) for k in range(1, members)]
    group_peers = [lax.rem(g + k, shares) for k in range(1, shares)]

    barrier = pltpu.get_barrier_semaphore()
    for peer in concept_peers:
        pl.semaphore_signal(
            barrier, inc=1, device_id={"concept": peer}, device_id_type=pl.DeviceIdType.MESH
        )
    for peer in group_peers:
        pl.semaphore_signal(
            barrier, inc=1, device_id={"group": peer}, device_id_type=pl.DeviceIdType.MESH
        )
    pl.semaphore_wait(barrier, members + shares - 2)

    def remote(source, target, send, recv, axis, peer):
        return pltpu.make_async_remote_copy(
            src_ref=source,
            dst_ref=target,
            send_sem=send,
            recv_sem=recv,
            device_id={axis: peer},
            device_id_type=pl.DeviceIdType.MESH,
        )

    lat[g, c] = latent_ref[0]
    first = [
        remote(lat.at[g, c], lat.at[g, c], lat_send.at[k], lat_recv.at[k], "concept", peer)
        for k, peer in enumerate(concept_peers)
    ]
    for copy in first:
        copy.start()
    for copy in first:
        copy.wait()
    second = [
        remote(lat.at[g], lat.at[g], line_send.at[k], line_recv.at[k], "group", peer)
        for k, peer in enumerate(group_peers)
    ]
    for copy in second:
        copy.start()
    for copy in second:
        copy.wait()

    gain_first = gain_in_ref[...]
    pull = gain_out_ref[...] * head_ref[...]
    pull_mean = jnp.mean(pull, axis=-1, keepdims=True)
    width = pull.shape[1]

    def forward(j):
        parts = []
        for s in range(PER_CHUNK):
            at = slot_ref[j * PER_CHUNK + s]
            parts.append(lat[at // members, lax.rem(at, members)])
        tokens = jnp.concatenate(parts, axis=0)
        base = jnp.dot(tokens, embed_ref[...], preferred_element_type=jnp.float32)
        normed_in, inverse_in = norm_forward(base)
        normed[j] = normed_in
        inverse[j] = inverse_in
        scaled = (normed_in * gain_first).astype(jnp.bfloat16)
        pre_act = jnp.dot(scaled, up_ref[...], preferred_element_type=jnp.float32)
        activated, slope = gelu_pair(pre_act)
        slopes[j] = slope
        partial = jnp.dot(
            activated.astype(jnp.bfloat16), down_ref[...], preferred_element_type=jnp.float32
        )
        own[j] = partial.astype(jnp.bfloat16)
        whole[j] = base + partial

    def right_copy(source, j):
        return remote(
            source, from_left.at[j], right_send.at[j], right_recv.at[j], "group", g + 1
        )

    def left_copy(source, j):
        return remote(
            source, from_right.at[j], left_send.at[j], left_recv.at[j], "group", g - 1
        )

    def pass_right(j):
        @pl.when(g == 0)
        def _():
            right_copy(own.at[j], j).start()

        @pl.when(g > 0)
        def _():
            pltpu.make_async_copy(from_left.at[j], from_left.at[j], right_recv.at[j]).wait()
            arrived = from_left[j].astype(jnp.float32)

            @pl.when(g < shares - 1)
            def _():
                to_right[j] = (own[j].astype(jnp.float32) + arrived).astype(jnp.bfloat16)
                right_copy(to_right.at[j], j).start()

            whole[j] += arrived

    def pass_left(j):
        @pl.when(g == shares - 1)
        def _():
            left_copy(own.at[j], j).start()

        @pl.when(g < shares - 1)
        def _():
            pltpu.make_async_copy(from_right.at[j], from_right.at[j], left_recv.at[j]).wait()
            arrived = from_right[j].astype(jnp.float32)

            @pl.when(g > 0)
            def _():
                to_left[j] = (own[j].astype(jnp.float32) + arrived).astype(jnp.bfloat16)
                left_copy(to_left.at[j], j).start()

            whole[j] += arrived

    share = jnp.where(g == 0, 1.0, 0.0)

    def backward(j):
        normed_out, inverse_out = norm_forward(whole[j])
        pulled = jnp.sum(normed_out * pull, axis=-1, keepdims=True)
        parts = []
        for s in range(PER_CHUNK):
            rows = slice(s * patches, (s + 1) * patches)
            logit = jnp.sum(pulled[rows], axis=0, keepdims=True) / patches
            factor = jax.nn.sigmoid(-logit) / patches
            parts.append(
                (factor * inverse_out[rows])
                * (pull - pull_mean - normed_out[rows] * (pulled[rows] / width))
            )
        back_res = jnp.concatenate(parts, axis=0)
        back_hidden = (
            contract_last(back_res.astype(jnp.bfloat16), down_ref[...]) * slopes[j]
        ).astype(jnp.bfloat16)
        back_scaled = contract_last(back_hidden, up_ref[...])
        back_base = (
            share * back_res + norm_backward(back_scaled * gain_first, normed[j], inverse[j])
        ).astype(jnp.bfloat16)
        result = contract_last(back_base, embed_ref[...])
        for s in range(PER_CHUNK):
            grads[j * PER_CHUNK + s] = result[s * patches : (s + 1) * patches]

    @pl.loop(0, chunks + shares)
    def _(t):
        right_at = t - g - 1
        left_at = t - (shares - g)

        @pl.when((right_at >= 0) & (right_at < chunks))
        def _():
            pass_right(right_at)

        @pl.when((left_at >= 0) & (left_at < chunks))
        def _():
            pass_left(left_at)

        @pl.when(t >= shares)
        def _():
            backward(t - shares)

        @pl.when(t < chunks)
        def _():
            forward(t)

    @pl.loop(0, members * shares)
    def _(at):
        spread[at // shares, lax.rem(at, shares)] = grads[back_slot_ref[at]] * back_mask_ref[at]

    third = [
        remote(spread.at[peer], met.at[k], back_send.at[k], back_recv.at[k], "concept", peer)
        for k, peer in enumerate(concept_peers)
    ]
    for copy in third:
        copy.start()
    total = spread[c]
    for k, copy in enumerate(third):
        copy.wait_recv()
        total = total + met[k]
    column[...] = total
    fourth = [
        remote(column.at[peer], ends.at[k], end_send.at[k], end_recv.at[k], "group", peer)
        for k, peer in enumerate(group_peers)
    ]
    for copy in fourth:
        copy.start()
    final = column[g]
    for k, copy in enumerate(fourth):
        copy.wait_recv()
        final = final + ends[k]
    out_ref[0] = final * strength_ref[0]

    for copy in third + fourth:
        copy.wait_send()

    @pl.loop(0, chunks)
    def _(j):
        @pl.when(g < shares - 1)
        def _():
            right_copy(own.at[j], j).wait_send()

        @pl.when(g > 0)
        def _():
            left_copy(own.at[j], j).wait_send()


def body(
    latents,
    concept_lists,
    list_length,
    concept_owner,
    strength,
    embed,
    gain_in,
    w_up,
    w_down,
    gain_out,
    w_head,
):
    here_concept = lax.axis_index("concept")
    members = lax.axis_size("concept")
    shares = lax.axis_size("group")
    image_count, patches, channels = latents.shape
    images = concept_lists.shape[0]
    width, hidden = w_up.shape[1], w_up.shape[2]
    owners, active = entry_owners(concept_lists, list_length, concept_owner)
    targets = jnp.arange(members, dtype=jnp.int32)
    named = jnp.any((owners[:, :, None] == targets) & active[:, :, None], axis=1).astype(jnp.int32)
    most = jnp.max(jnp.sum(named, axis=0))
    mine = jnp.sum(jnp.where(targets == here_concept, named, 0), axis=1)
    image_ids = jnp.arange(images, dtype=jnp.int32)
    earlier = (image_ids[:, None] < image_ids[None, :]).astype(jnp.int32)
    ranks = jnp.sum(earlier * mine[:, None], axis=0)
    places = lax.rem(image_ids, shares) * members + image_ids // shares

    def run(slots, start, number):
        ids = jnp.arange(slots, dtype=jnp.int32) + start
        chosen = (ids[:, None] == ranks[None, :]) & (mine > 0)[None, :]
        slot_places = jnp.sum(jnp.where(chosen, places[None, :], 0), axis=1)
        inside = (mine > 0) & (ranks >= start) & (ranks < start + slots)
        back_slots = jnp.where(inside, ranks - start, 0)
        chunks, rows = slots // PER_CHUNK, PER_CHUNK * patches
        block = (chunks, rows, width)
        vmem = pl.BlockSpec(memory_space=pltpu.VMEM)
        smem = pl.BlockSpec(memory_space=pltpu.SMEM)
        piece = (patches, channels)
        dma = pltpu.SemaphoreType.DMA
        return pl.pallas_call(
            functools.partial(guide_kernel, chunks, members, shares),
            out_shape=jax.ShapeDtypeStruct(latents.shape, jnp.float32),
            in_specs=[smem] * 4 + [vmem] * 7,
            out_specs=vmem,
            scratch_shapes=[
                pltpu.VMEM((shares, members) + piece, jnp.bfloat16),
                pltpu.VMEM(block, jnp.float32),
                pltpu.VMEM(block, jnp.float32),
                pltpu.VMEM((chunks, rows, 1), jnp.float32),
                pltpu.VMEM((chunks, rows, hidden), jnp.float32),
                pltpu.VMEM(block, jnp.bfloat16),
                pltpu.VMEM(block, jnp.bfloat16),
                pltpu.VMEM(block, jnp.bfloat16),
                pltpu.VMEM(block, jnp.bfloat16),
                pltpu.VMEM(block, jnp.bfloat16),
                pltpu.VMEM((slots,) + piece, jnp.float32),
                pltpu.VMEM((members, shares) + piece, jnp.float32),
                pltpu.VMEM((members - 1, shares) + piece, jnp.float32),
                pltpu.VMEM((shares,) + piece, jnp.float32),
                pltpu.VMEM((shares - 1,) + piece, jnp.float32),
                dma((members - 1,)),
                dma((members - 1,)),
                dma((shares - 1,)),
                dma((shares - 1,)),
                dma((chunks,)),
                dma((chunks,)),
                dma((chunks,)),
                dma((chunks,)),
                dma((members - 1,)),
                dma((members - 1,)),
                dma((shares - 1,)),
                dma((shares - 1,)),
            ],
            compiler_params=pltpu.CompilerParams(
                collective_id=number, has_side_effects=True, vmem_limit_bytes=56 * 1024 * 1024
            ),
        )(
            slot_places,
            back_slots,
            inside.astype(jnp.float32),
            strength,
            latents,
            embed[0],
            gain_in,
            w_up[0],
            w_down[0],
            gain_out,
            w_head,
        )

    room = 32
    if images <= room:
        small = max(PER_CHUNK, 3 * images // 4 // PER_CHUNK * PER_CHUNK)
        return lax.cond(
            most <= small, lambda: run(small, 0, 0), lambda: run(images, 0, 1)
        )
    rounds = (images + room - 1) // room
    return lax.fori_loop(
        0,
        rounds,
        lambda turn, total: total + run(room, turn * room, 0),
        jnp.zeros(latents.shape, jnp.float32),
    )


def solution(mesh):
    in_specs = (
        P(("concept", "group"), None, None),
        P(),
        P(),
        P(),
        P(("concept", "group")),
        P("concept", None, None),
        P("concept", None),
        P("concept", None, "group"),
        P("concept", "group", None),
        P("concept", None),
        P("concept", None),
    )
    out_specs = P(("concept", "group"), None, None)
    return jax.shard_map(body, mesh=mesh, in_specs=in_specs, out_specs=out_specs, check_vma=False)
```

```python
import functools

import jax
import jax.numpy as jnp
from jax import lax
from jax.experimental import pallas as pl
from jax.experimental.pallas import tpu as pltpu
from jax.sharding import PartitionSpec as P


def norm_forward(values):
    center = jnp.mean(values, axis=-1, keepdims=True)
    shifted = values - center
    variance = jnp.mean(shifted * shifted, axis=-1, keepdims=True)
    inverse = lax.rsqrt(variance + 1e-05)
    return (shifted * inverse, inverse)


def norm_backward(upstream, normed, inverse):
    return inverse * (
        upstream
        - jnp.mean(upstream, axis=-1, keepdims=True)
        - normed * jnp.mean(upstream * normed, axis=-1, keepdims=True)
    )


def gelu_pair(pre_act):
    cumulative = 0.5 * (1.0 + lax.erf(pre_act * 0.7071067811865476))
    return (
        pre_act * cumulative,
        cumulative + pre_act * jnp.exp(-0.5 * pre_act * pre_act) * 0.3989422804014327,
    )


def entry_owners(lists, lengths, owner_table):
    concept_ids = jnp.arange(owner_table.shape[0], dtype=jnp.int32)
    owners = jnp.sum(jnp.where(lists[:, :, None] == concept_ids, owner_table, 0), axis=2)
    active = jnp.arange(lists.shape[1], dtype=jnp.int32)[None, :] < lengths[:, None]
    return (owners, active)


def contract_last(left, right):
    return lax.dot_general(
        left, right, (((1,), (1,)), ((), ())), preferred_element_type=jnp.float32
    )


PER_CHUNK = 2
SIZES = (6, 7, 8, 10, 16)


def guide_kernel(
    chunks,
    members,
    shares,
    slot_ref,
    which_ref,
    back_slot_ref,
    back_mask_ref,
    strength_ref,
    latent_ref,
    embed_ref,
    gain_in_ref,
    up_ref,
    down_ref,
    gain_out_ref,
    head_ref,
    out_ref,
    ups,
    downs,
    embeds,
    vectors,
    lat,
    whole,
    normed,
    inverse,
    slopes,
    own,
    to_right,
    to_left,
    from_left,
    from_right,
    grads,
    spread,
    met,
    column,
    ends,
    keep,
    share_send,
    share_recv,
    lat_send,
    lat_recv,
    line_send,
    line_recv,
    right_send,
    right_recv,
    left_send,
    left_recv,
    back_send,
    back_recv,
    end_send,
    end_recv,
):
    c = lax.axis_index("concept")
    g = lax.axis_index("group")
    patches = latent_ref.shape[1]
    concept_peers = [lax.rem(c + k, members) for k in range(1, members)]
    group_peers = [lax.rem(g + k, shares) for k in range(1, shares)]

    barrier = pltpu.get_barrier_semaphore()
    for peer in concept_peers:
        pl.semaphore_signal(
            barrier, inc=1, device_id={"concept": peer}, device_id_type=pl.DeviceIdType.MESH
        )
    for peer in group_peers:
        pl.semaphore_signal(
            barrier, inc=1, device_id={"group": peer}, device_id_type=pl.DeviceIdType.MESH
        )
    pl.semaphore_wait(barrier, members + shares - 2)

    def remote(source, target, send, recv, axis, peer):
        return pltpu.make_async_remote_copy(
            src_ref=source,
            dst_ref=target,
            send_sem=send,
            recv_sem=recv,
            device_id={axis: peer},
            device_id_type=pl.DeviceIdType.MESH,
        )

    side = lax.rem(c, 2)
    partner = c + 1 - 2 * side
    vectors[side] = jnp.zeros(vectors.shape[1:], jnp.float32)
    vectors[side, 0:1] = gain_in_ref[...]
    vectors[side, 1:2] = gain_out_ref[...] * head_ref[...]
    kept, shared = [], []
    for k, (source, both) in enumerate(
        ((embed_ref, embeds), (vectors.at[side], vectors), (up_ref, ups), (down_ref, downs))
    ):
        if both is not vectors:
            kept.append(pltpu.make_async_copy(source, both.at[side], keep.at[k]))
        shared.append(
            remote(source, both.at[side], share_send.at[k], share_recv.at[k], "concept", partner)
        )
    lat[g, c] = latent_ref[0]
    first = [
        remote(lat.at[g, c], lat.at[g, c], lat_send.at[k], lat_recv.at[k], "concept", peer)
        for k, peer in enumerate(concept_peers)
    ]
    for copy in first + kept + shared:
        copy.start()
    for copy in first:
        copy.wait()
    second = [
        remote(lat.at[g], lat.at[g], line_send.at[k], line_recv.at[k], "group", peer)
        for k, peer in enumerate(group_peers)
    ]
    for copy in second:
        copy.start()
    for copy in second:
        copy.wait()

    for copy in kept + shared:
        copy.wait()
    width = up_ref.shape[0]

    def forward(j):
        own_one = which_ref[j]
        gain_first = vectors[own_one][0:1]
        parts = []
        for s in range(PER_CHUNK):
            at = slot_ref[j * PER_CHUNK + s]
            parts.append(lat[at // members, lax.rem(at, members)])
        tokens = jnp.concatenate(parts, axis=0)
        base = jnp.dot(tokens, embeds[own_one], preferred_element_type=jnp.float32)
        normed_in, inverse_in = norm_forward(base)
        normed[j] = normed_in
        inverse[j] = inverse_in
        scaled = (normed_in * gain_first).astype(jnp.bfloat16)
        pre_act = jnp.dot(scaled, ups[own_one], preferred_element_type=jnp.float32)
        activated, slope = gelu_pair(pre_act)
        slopes[j] = slope
        partial = jnp.dot(
            activated.astype(jnp.bfloat16), downs[own_one], preferred_element_type=jnp.float32
        )
        own[j] = partial.astype(jnp.bfloat16)
        whole[j] = base + partial

    def right_copy(source, j):
        return remote(
            source, from_left.at[j], right_send.at[j], right_recv.at[j], "group", g + 1
        )

    def left_copy(source, j):
        return remote(
            source, from_right.at[j], left_send.at[j], left_recv.at[j], "group", g - 1
        )

    def pass_right(j):
        @pl.when(g == 0)
        def _():
            right_copy(own.at[j], j).start()

        @pl.when(g > 0)
        def _():
            pltpu.make_async_copy(from_left.at[j], from_left.at[j], right_recv.at[j]).wait()
            arrived = from_left[j].astype(jnp.float32)

            @pl.when(g < shares - 1)
            def _():
                to_right[j] = (own[j].astype(jnp.float32) + arrived).astype(jnp.bfloat16)
                right_copy(to_right.at[j], j).start()

            whole[j] += arrived

    def pass_left(j):
        @pl.when(g == shares - 1)
        def _():
            left_copy(own.at[j], j).start()

        @pl.when(g < shares - 1)
        def _():
            pltpu.make_async_copy(from_right.at[j], from_right.at[j], left_recv.at[j]).wait()
            arrived = from_right[j].astype(jnp.float32)

            @pl.when(g > 0)
            def _():
                to_left[j] = (own[j].astype(jnp.float32) + arrived).astype(jnp.bfloat16)
                left_copy(to_left.at[j], j).start()

            whole[j] += arrived

    share = jnp.where(g == 0, 1.0, 0.0)

    def backward(j):
        own_one = which_ref[j]
        gain_first = vectors[own_one][0:1]
        pull = vectors[own_one][1:2]
        pull_mean = jnp.mean(pull, axis=-1, keepdims=True)
        normed_out, inverse_out = norm_forward(whole[j])
        pulled = jnp.sum(normed_out * pull, axis=-1, keepdims=True)
        parts = []
        for s in range(PER_CHUNK):
            rows = slice(s * patches, (s + 1) * patches)
            logit = jnp.sum(pulled[rows], axis=0, keepdims=True) / patches
            factor = jax.nn.sigmoid(-logit) / patches
            parts.append(
                (factor * inverse_out[rows])
                * (pull - pull_mean - normed_out[rows] * (pulled[rows] / width))
            )
        back_res = jnp.concatenate(parts, axis=0)
        back_hidden = (
            contract_last(back_res.astype(jnp.bfloat16), downs[own_one]) * slopes[j]
        ).astype(jnp.bfloat16)
        back_scaled = contract_last(back_hidden, ups[own_one])
        back_base = (
            share * back_res + norm_backward(back_scaled * gain_first, normed[j], inverse[j])
        ).astype(jnp.bfloat16)
        result = contract_last(back_base, embeds[own_one])
        for s in range(PER_CHUNK):
            grads[j * PER_CHUNK + s] = result[s * patches : (s + 1) * patches]

    @pl.loop(0, chunks + shares)
    def _(t):
        right_at = t - g - 1
        left_at = t - (shares - g)

        @pl.when((right_at >= 0) & (right_at < chunks))
        def _():
            pass_right(right_at)

        @pl.when((left_at >= 0) & (left_at < chunks))
        def _():
            pass_left(left_at)

        @pl.when(t >= shares)
        def _():
            backward(t - shares)

        @pl.when(t < chunks)
        def _():
            forward(t)

    @pl.loop(0, members * shares)
    def _(at):
        other = at + members * shares
        spread[at // shares, lax.rem(at, shares)] = (
            grads[back_slot_ref[at]] * back_mask_ref[at]
            + grads[back_slot_ref[other]] * back_mask_ref[other]
        )

    third = [
        remote(spread.at[peer], met.at[k], back_send.at[k], back_recv.at[k], "concept", peer)
        for k, peer in enumerate(concept_peers)
    ]
    for copy in third:
        copy.start()
    total = spread[c]
    for k, copy in enumerate(third):
        copy.wait_recv()
        total = total + met[k]
    column[...] = total
    fourth = [
        remote(column.at[peer], ends.at[k], end_send.at[k], end_recv.at[k], "group", peer)
        for k, peer in enumerate(group_peers)
    ]
    for copy in fourth:
        copy.start()
    final = column[g]
    for k, copy in enumerate(fourth):
        copy.wait_recv()
        final = final + ends[k]
    out_ref[0] = final * strength_ref[0]

    for copy in third + fourth:
        copy.wait_send()

    @pl.loop(0, chunks)
    def _(j):
        @pl.when(g < shares - 1)
        def _():
            right_copy(own.at[j], j).wait_send()

        @pl.when(g > 0)
        def _():
            left_copy(own.at[j], j).wait_send()


def body(
    latents,
    concept_lists,
    list_length,
    concept_owner,
    strength,
    embed,
    gain_in,
    w_up,
    w_down,
    gain_out,
    w_head,
):
    here_concept = lax.axis_index("concept")
    members = lax.axis_size("concept")
    shares = lax.axis_size("group")
    image_count, patches, channels = latents.shape
    images = concept_lists.shape[0]
    width, hidden = w_up.shape[1], w_up.shape[2]
    owners, active = entry_owners(concept_lists, list_length, concept_owner)
    targets = jnp.arange(members, dtype=jnp.int32)
    named = jnp.any((owners[:, :, None] == targets) & active[:, :, None], axis=1).astype(jnp.int32)
    side = lax.rem(here_concept, 2)
    loads = jnp.sum(named, axis=0)
    chunk_loads = (loads + PER_CHUNK - 1) // PER_CHUNK
    most = jnp.max(jnp.sum(chunk_loads.reshape(-1, 2), axis=1))
    pair = here_concept - side + jnp.arange(2, dtype=jnp.int32)
    mine = jnp.sum(jnp.where(targets[None, None, :] == pair[:, None, None], named[None], 0), axis=2)
    image_ids = jnp.arange(images, dtype=jnp.int32)
    earlier = image_ids[:, None] < image_ids[None, :]
    ranks = jnp.sum(jnp.where(earlier[None], mine[:, :, None], 0), axis=1)
    first_load = (jnp.sum(mine[0]) + PER_CHUNK - 1) // PER_CHUNK
    offsets = jnp.stack([jnp.zeros_like(first_load), first_load])
    chunk_of = ranks // PER_CHUNK + offsets[:, None]
    slot_of = jnp.where(
        (mine > 0) & (lax.rem(chunk_of, 2) == side),
        chunk_of // 2 * PER_CHUNK + lax.rem(ranks, PER_CHUNK),
        -1,
    )
    places = lax.rem(image_ids, shares) * members + image_ids // shares

    def run(chunks, start, number):
        slots, rows = chunks * PER_CHUNK, PER_CHUNK * patches
        local = jnp.where(slot_of >= start * PER_CHUNK, slot_of - start * PER_CHUNK, -1)
        ids = jnp.arange(slots, dtype=jnp.int32)
        chosen = ids[:, None, None] == local[None]
        slot_places = jnp.sum(jnp.where(chosen, places[None, None, :], 0), axis=(1, 2))
        turns = (jnp.arange(chunks, dtype=jnp.int32) + start) * 2 + side
        which = (turns >= first_load).astype(jnp.int32)
        inside = ((local >= 0) & (local < slots)).reshape(-1)
        back_slots = jnp.where(inside, local.reshape(-1), 0)
        block = (chunks, rows, width)
        vmem = pl.BlockSpec(memory_space=pltpu.VMEM)
        smem = pl.BlockSpec(memory_space=pltpu.SMEM)
        piece = (patches, channels)
        dma = pltpu.SemaphoreType.DMA
        return pl.pallas_call(
            functools.partial(guide_kernel, chunks, members, shares),
            out_shape=jax.ShapeDtypeStruct(latents.shape, jnp.float32),
            in_specs=[smem] * 5 + [vmem] * 7,
            out_specs=vmem,
            scratch_shapes=[
                pltpu.VMEM((2,) + w_up.shape[1:], jnp.bfloat16),
                pltpu.VMEM((2,) + w_down.shape[1:], jnp.bfloat16),
                pltpu.VMEM((2,) + embed.shape[1:], jnp.bfloat16),
                pltpu.VMEM((2, 8, width), jnp.float32),
                pltpu.VMEM((shares, members) + piece, jnp.bfloat16),
                pltpu.VMEM(block, jnp.float32),
                pltpu.VMEM(block, jnp.float32),
                pltpu.VMEM((chunks, rows, 1), jnp.float32),
                pltpu.VMEM((chunks, rows, hidden), jnp.float32),
                pltpu.VMEM(block, jnp.bfloat16),
                pltpu.VMEM(block, jnp.bfloat16),
                pltpu.VMEM(block, jnp.bfloat16),
                pltpu.VMEM(block, jnp.bfloat16),
                pltpu.VMEM(block, jnp.bfloat16),
                pltpu.VMEM((slots,) + piece, jnp.float32),
                pltpu.VMEM((members, shares) + piece, jnp.float32),
                pltpu.VMEM((members - 1, shares) + piece, jnp.float32),
                pltpu.VMEM((shares,) + piece, jnp.float32),
                pltpu.VMEM((shares - 1,) + piece, jnp.float32),
                dma((4,)),
                dma((4,)),
                dma((4,)),
                dma((members - 1,)),
                dma((members - 1,)),
                dma((shares - 1,)),
                dma((shares - 1,)),
                dma((chunks,)),
                dma((chunks,)),
                dma((chunks,)),
                dma((chunks,)),
                dma((members - 1,)),
                dma((members - 1,)),
                dma((shares - 1,)),
                dma((shares - 1,)),
            ],
            compiler_params=pltpu.CompilerParams(
                collective_id=number, has_side_effects=True, vmem_limit_bytes=56 * 1024 * 1024
            ),
        )(
            slot_places,
            which,
            back_slots,
            inside.astype(jnp.float32),
            strength,
            latents,
            embed[0],
            gain_in,
            w_up[0],
            w_down[0],
            gain_out,
            w_head,
        )

    worst = (images + PER_CHUNK - 1) // PER_CHUNK
    room = 32 // PER_CHUNK
    if worst <= room:
        sizes = sorted({max(1, worst * eighths // 16) for eighths in SIZES})
        choice = sum(((most + 1) // 2 > size).astype(jnp.int32) for size in sizes[:-1])
        return lax.switch(
            choice, [lambda n=n, size=size: run(size, 0, n) for n, size in enumerate(sizes)]
        )
    rounds = (worst + room - 1) // room
    return lax.fori_loop(
        0,
        rounds,
        lambda turn, total: total + run(room, turn * room, 0),
        jnp.zeros(latents.shape, jnp.float32),
    )


def solution(mesh):
    in_specs = (
        P(("concept", "group"), None, None),
        P(),
        P(),
        P(),
        P(("concept", "group")),
        P("concept", None, None),
        P("concept", None),
        P("concept", None, "group"),
        P("concept", "group", None),
        P("concept", None),
        P("concept", None),
    )
    out_specs = P(("concept", "group"), None, None)
    return jax.shard_map(body, mesh=mesh, in_specs=in_specs, out_specs=out_specs, check_vma=False)
```
